128 devices in a mesh: batch: 8 (over y, core), tensor: 16 (over z, x).
Axes of the slice: x: 4, y: 4, z: 4, core: 2. Of those that a mesh axis runs over, the one named last changes fastest.
Arguments:
- tokens: bfloat16 [32768, 1024], P(('batch', 'tensor')), may hold values from -6 to 6
- gain_attn: float32 [1024], replicated, may hold values from 0.1 to 1.9
- w_qkv: bfloat16 [1024, 3072], P('batch', 'tensor'), may hold values from -0.1875 to 0.1875
- w_attn_out: bfloat16 [1024, 1024], P('batch', 'tensor'), may hold values from -0.1875 to 0.1875
- kv_cache: bfloat16 [1024, 128, 2048], P('batch', None, 'tensor'), may hold values from -192 to 192
- page_table: int32 [8, 128], P('batch'), may hold values from 0 to 127, each once within a row
- cached_lengths: int32 [32], P('batch'), may hold values from 1 to 4096, 32768 in all
- gain_moe: float32 [1024], replicated, may hold values from 0.1 to 1.9
- w_router: bfloat16 [1024, 16], replicated, may hold values from -0.1875 to 0.1875
- routes: int32 [32768, 2], P(('batch', 'tensor')), may hold values from 0 to 15, all different within a row; in each aligned block of 256 rows (0 to 255, 256 to 511, ...) at most 40 rows name the same one
- w_in: bfloat16 [16, 1024, 5632], P('tensor'), may hold values from -0.1875 to 0.1875
- w_out: bfloat16 [16, 2816, 1024], P('tensor'), may hold values from -0.109375 to 0.109375
Outputs:
- mixed: bfloat16 [32768, 1024], P(('batch', 'tensor'))
The draws below stay inside these ranges and needn't reach their ends.
Inputs may be any that keep to these rules, and one draw needn't show every extreme that they name: `page_table`: each row lists all 128 pages of one batch index's pool once; local request r of that batch index reads its cached tokens from entries r * 32 to (r + 1) * 32 - 1 in order. `cached_lengths`: they sum to 32768. `routes`: a token's 2 experts differ; in the rows of one device (256 aligned rows) no expert is named by more than 40 rows, a bound that some block reaches.
All inputs are finite; a program needn't handle non-finite values. No bound on the sum of `cached_lengths` on one device may be relied on, other than what follows from the above.
Results may differ from the reference program's by a relative error of at most 0.012.
Values may be sent and summed in bfloat16 or wider, within the bound.
A program may use at most 128 MiB of HBM per device.

```python
import math
import jax
import jax.numpy as jnp
import numpy as np
from jax import lax

D = 1024
HD = 64
FF = 2816
TOP = 2
R = 4
SPAN = 1024
PAGE = 128
CACHE_MAX = 4096
CACHE_MEAN = 1024
HEADS = 16
EXPERTS = 16
GROUPS = 8
REQUESTS = 32
TOK_DEV = 256
TOKENS = 32768
MAXPAGES = 32
POOL = 128
CAP = 40


def draw_kv_cache(key, part):
    values = jax.random.normal(jax.random.fold_in(key, 11), (GROUPS * POOL, PAGE, HEADS, 2, HD), jnp.float32)
    values = jnp.clip(values, -4.0, 4.0)
    return values.reshape(GROUPS * POOL, PAGE, HEADS * 2 * HD).astype(jnp.bfloat16)


def block_levels(rng, shape, pieces, smallest, largest):
    level = 1.0
    for axis_at, parts in pieces:
        heights = jax.random.uniform(jax.random.fold_in(jax.random.fold_in(rng, 6), axis_at), (parts,), jnp.float32, smallest / len(pieces), largest / len(pieces))
        level = level * jnp.repeat(jnp.exp(heights), shape[axis_at] // parts).reshape((-1,) + (1,) * (len(shape) - 1 - axis_at))
    return level


def split_up(count, total, limit, slope):
    portions = [(1 << 20) // math.isqrt(rank ** slope) + 1 for rank in range(2, count + 1)]
    rest, counts = total - limit - (count - 1), [1] * (count - 1)
    while rest > 0:
        candidates = [i for i in range(count - 1) if counts[i] < limit]
        whole, left = sum([portions[i] for i in candidates]), rest
        for i in candidates:
            addition = min(limit - counts[i], max(1, left * portions[i] // whole), rest)
            counts[i] = counts[i] + addition
            rest = rest - addition
    return np.array([limit] + counts)


def uneven(key, number_of, total, bound, skew):
    if number_of == 2:
        one = jax.random.randint(key, (), max(1, total - bound), min(bound, total - 1) + 1)
        return jnp.stack([one, total - one])
    sizes = jnp.asarray(split_up(number_of, total, bound, skew), jnp.int32)
    pairs = (number_of - 1) // 2
    donor, receiver = sizes[1:1 + 2 * pairs:2], sizes[2:2 + 2 * pairs:2]
    slack = jnp.minimum(donor - 1, bound - receiver)
    passed = jax.random.randint(jax.random.fold_in(key, 1), (pairs,), 0, 1 << 20) % (slack + 1)
    sizes = sizes.at[1:1 + 2 * pairs:2].set(donor - passed).at[2:2 + 2 * pairs:2].set(receiver + passed)
    return sizes[jax.random.permutation(jax.random.fold_in(key, 2), number_of)]


def deal_out(key, own, number, rows, amount, top, limit, skew):
    sequence = jax.random.permutation(key, amount)
    packed, usual = load_shares(amount, rows * top, limit, skew, True), load_shares(amount, rows * top, limit, skew, False)
    places = jnp.arange(amount)

    def named(lengths, offset_by):
        used = int((lengths > 0).sum())
        fixed = max(1, used // 4)
        passed = fixed + (places - fixed + offset_by * (used - fixed)) % max(1, amount - fixed)
        return jnp.zeros((amount,), jnp.int32).at[sequence[jnp.where(places < fixed, places, passed)]].set(jnp.asarray(lengths, jnp.int32))

    lengths = jnp.where(number % 4 == 0, named(packed, number // 4), named(usual, number - number // 4 - 1))
    mixed = jax.random.permutation(jax.random.fold_in(own, 3), amount)
    donor, receiver = mixed[0:amount // 2 * 2:2], mixed[1:amount // 2 * 2:2]
    room = jnp.minimum(lengths[donor] - 1, limit - lengths[receiver]) // 2
    room = jnp.where((donor == sequence[0]) | (receiver == sequence[0]) | (lengths[receiver] == 0), 0, jnp.maximum(room, 0))
    passed = jax.random.randint(jax.random.fold_in(own, 4), (amount // 2,), 0, 1 << 20) % (room + 1)
    lengths = lengths.at[donor].add(-passed).at[receiver].add(passed)
    members = jnp.searchsorted(jnp.cumsum(lengths), jnp.arange(rows * top), side="right").astype(jnp.int32)
    grid = members.reshape(top, rows).T
    grid = grid[jax.random.permutation(jax.random.fold_in(own, 1), rows)]
    offset_by = jax.random.randint(jax.random.fold_in(own, 2), (rows, 1), 0, top)
    return jnp.take_along_axis(grid, (jnp.arange(top)[None, :] + offset_by) % top, axis=1)


def load_shares(number_of, total, limit, lean, full):
    weights = [(1 << 20) // math.isqrt(standing ** lean) + 1 for standing in range(1, number_of + 1)]
    largest = limit if full else min(limit, max(-(-total // number_of), total * weights[0] // sum(weights)))
    least = 1 if total - largest >= number_of - 1 else 0
    holding, spare = [largest] + [least] * (number_of - 1), total - largest - least * (number_of - 1)
    while spare > 0:
        movable = [i for i in range(1, number_of) if holding[i] < largest] or [i for i in range(1, number_of) if holding[i] < limit]
        pool, budget = sum([weights[i] for i in movable]), spare
        for i in movable:
            extra = min(limit - holding[i], max(1, budget * weights[i] // pool), spare)
            holding[i] = holding[i] + extra
            spare = spare - extra
    return np.array(holding)


def centred(rng, dims, width, limit, shards=(), kind=jnp.bfloat16):
    level = block_levels(rng, dims, shards, -0.22, 0.18) if shards else 1.0
    entries = jax.random.normal(rng, dims, jnp.float32) * width * level
    return jnp.minimum(jnp.maximum(entries, -limit), limit).astype(kind)


def setup_inputs(seed: int = 0) -> dict:
    seeds = jax.random.split(jax.random.key(seed), 13)
    tokens = centred(seeds[0], (TOKENS, D), 1.0, 6.0, ((0, 128),))
    gain_attn = jnp.clip(1.0 + 0.18 * jax.random.normal(seeds[1], (D,), jnp.float32), 0.1, 1.9)
    w_qkv = centred(seeds[2], (D, HEADS * 3 * HD), D ** -0.5, 0.1875, ((0, 8), (1, 16)))
    w_attn_out = centred(seeds[3], (D, HEADS * HD), (HEADS * HD) ** -0.5, 0.1875, ((0, 8), (1, 16)))
    kv_cache = draw_kv_cache(jax.random.fold_in(seeds[12], 71), 0)
    page_table = jax.vmap(lambda own: jax.random.permutation(own, POOL))(jax.random.split(seeds[5], GROUPS)).reshape((GROUPS, POOL)).astype(jnp.int32)
    cached_lengths = uneven(seeds[6], REQUESTS, REQUESTS * CACHE_MEAN, CACHE_MAX, 2).astype(jnp.int32)
    gain_moe = jnp.clip(1.0 + 0.18 * jax.random.normal(seeds[7], (D,), jnp.float32), 0.1, 1.9)
    w_router = centred(seeds[8], (D, EXPERTS), D ** -0.5, 0.1875)
    routes_keys = jax.random.split(jax.random.fold_in(seeds[9], 1), TOKENS // TOK_DEV)
    routes_turns = jax.random.permutation(jax.random.fold_in(seeds[9], 3), TOKENS // TOK_DEV)
    routes = jax.vmap(lambda own, number: deal_out(jax.random.fold_in(seeds[9], 2), own, number, TOK_DEV, EXPERTS, TOP, CAP, 2))(routes_keys, routes_turns).reshape((TOKENS, TOP))
    w_in = centred(seeds[10], (EXPERTS, D, 2 * FF), D ** -0.5, 0.1875, ((0, 16),))
    w_out = centred(seeds[11], (EXPERTS, FF, D), FF ** -0.5, 0.109375, ((0, 16),))
    return {"tokens": tokens, "gain_attn": gain_attn, "w_qkv": w_qkv, "w_attn_out": w_attn_out, "kv_cache": kv_cache, "page_table": page_table, "cached_lengths": cached_lengths, "gain_moe": gain_moe, "w_router": w_router, "routes": routes, "w_in": w_in, "w_out": w_out}


EPSILON = 1e-06
NEGATIVE = -1e+30

def rms_norm(values, gain):
    values = values.astype(jnp.float32)
    mean_square = lax.optimization_barrier(jnp.mean(values * values, axis=-1, keepdims=True))
    return values * lax.rsqrt(mean_square + EPSILON) * gain.astype(jnp.float32)

def reference(tokens, gain_attn, w_qkv, w_attn_out, kv_cache, page_table, cached_lengths, gain_moe, w_router, routes, w_in, w_out):
    normed = rms_norm(tokens, gain_attn).astype(jnp.bfloat16)
    projected = jnp.dot(normed, w_qkv, preferred_element_type=jnp.float32).astype(jnp.bfloat16)
    heads_all = w_attn_out.shape[1] // HD
    scale = 1.0 / math.sqrt(HD)
    column = jnp.arange(CACHE_MAX + SPAN, dtype=jnp.int32)
    line = jnp.arange(SPAN, dtype=jnp.int32)

    def one_request(request):
        group = request // R
        local = request % R
        block = lax.dynamic_slice_in_dim(projected, (request * SPAN).astype(jnp.int32), SPAN, 0)
        block = block.reshape(SPAN, heads_all, 3, HD).astype(jnp.float32)
        pages = lax.dynamic_slice_in_dim(page_table[group], (local * MAXPAGES).astype(jnp.int32), MAXPAGES, 0)
        cached = kv_cache[group * POOL + pages].reshape(CACHE_MAX, heads_all, 2, HD).astype(jnp.float32)
        keys = jnp.concatenate([cached[:, :, 0], block[:, :, 1]], axis=0)
        values_all = jnp.concatenate([cached[:, :, 1], block[:, :, 2]], axis=0)
        scores = jnp.einsum('qhd,khd->hqk', block[:, :, 0], keys) * scale
        visible = jnp.where(column[None, :] < CACHE_MAX, column[None, :] < cached_lengths[request], column[None, :] - CACHE_MAX <= line[:, None])
        scores = jnp.where(visible[None], scores, NEGATIVE)
        top_score = lax.optimization_barrier(jnp.max(scores, axis=2, keepdims=True))
        weights = jnp.exp(scores - top_score)
        weights = (weights / lax.optimization_barrier(jnp.sum(weights, axis=2, keepdims=True))).astype(jnp.bfloat16)
        outcome = jnp.einsum('hqk,khd->qhd', weights.astype(jnp.float32), values_all).astype(jnp.bfloat16)
        return outcome.reshape(SPAN, heads_all * HD)
    attended = lax.map(one_request, jnp.arange(REQUESTS, dtype=jnp.int32)).reshape(TOKENS, heads_all * HD)
    projection = jnp.dot(attended, w_attn_out.T, preferred_element_type=jnp.float32)
    state = tokens.astype(jnp.float32) + projection
    normed_moe = rms_norm(state, gain_moe).astype(jnp.bfloat16)
    logits = jnp.dot(normed_moe, w_router, preferred_element_type=jnp.float32)
    picked = jnp.take_along_axis(logits, routes, axis=1)
    squashed = jax.nn.sigmoid(picked)
    gates = squashed / lax.optimization_barrier(jnp.sum(squashed, axis=1, keepdims=True))
    experts = w_router.shape[1]
    blocks = TOKENS // TOK_DEV
    flat_routes = routes.reshape(blocks, TOK_DEV * TOP)
    onehot = (flat_routes[..., None] == jnp.arange(experts, dtype=jnp.int32)).astype(jnp.int32)
    before = jnp.cumsum(onehot, axis=1) - onehot
    slots = lax.optimization_barrier(jnp.sum(before * onehot, axis=-1)).astype(jnp.int32)
    owner_rows = jnp.broadcast_to(jnp.arange(TOK_DEV * TOP, dtype=jnp.int32) // TOP, (blocks, TOK_DEV * TOP))
    flat_gates = gates.reshape(blocks, TOK_DEV * TOP)
    padded = jnp.concatenate([normed_moe.reshape(blocks, TOK_DEV, D), jnp.zeros((blocks, 1, D), jnp.bfloat16)], axis=1)
    block_index = jnp.arange(blocks, dtype=jnp.int32)[:, None]

    def one_expert(total, inputs):
        expert, gate_up, down = inputs
        target = jnp.where(flat_routes == expert, slots, CAP).astype(jnp.int32)
        sources = jnp.full((blocks, CAP), TOK_DEV, jnp.int32).at[block_index, target].set(owner_rows, mode='drop')
        slot_gates = jnp.zeros((blocks, CAP), jnp.float32).at[block_index, target].set(flat_gates, mode='drop')
        gathered = padded[block_index, sources].reshape(blocks * CAP, D)
        inner = jnp.dot(gathered, gate_up, preferred_element_type=jnp.float32)
        active = (jax.nn.gelu(inner[:, :FF], approximate=True) * inner[:, FF:]).astype(jnp.bfloat16)
        outcome = jnp.dot(active, down, preferred_element_type=jnp.float32).astype(jnp.bfloat16).reshape(blocks, CAP, D)
        total = total.at[block_index, sources].add(slot_gates[..., None] * outcome.astype(jnp.float32))
        return (total, None)
    start_total = jnp.zeros((blocks, TOK_DEV + 1, D), jnp.float32)
    total, unused = lax.scan(one_expert, start_total, (jnp.arange(experts, dtype=jnp.int32), w_in, w_out))
    return (state + total[:, :TOK_DEV].reshape(TOKENS, D)).astype(jnp.bfloat16)
```

```python
import math

import jax
import jax.numpy as jnp
from jax import lax
from jax.experimental import pallas as pl
from jax.experimental.pallas import tpu as pltpu
from jax.sharding import PartitionSpec as P

HD = 64


EPSILON = 1e-06
NEGATIVE = -1e30
CONTRACT = (((1,), (1,)), ((), ()))


def rms_norm(values, gain):
    values = values.astype(jnp.float32)
    mean_square = jnp.mean(values * values, axis=-1, keepdims=True)
    return values * lax.rsqrt(mean_square + EPSILON) * gain


PAGE = 128
TQ = 256
CK = 512


def attention_kernel(table, lengths, q_ref, kv_ref, cache_ref, out_ref, pages, top, total, sems):
    requests, per_request = pages.shape[0], pages.shape[1] // PAGE
    span = q_ref.shape[0] // requests
    tiles = span // TQ

    def fetch(entry):
        return pltpu.make_async_copy(
            cache_ref.at[table[entry]],
            pages.at[entry // per_request, pl.ds((entry % per_request) * PAGE, PAGE), :],
            sems.at[entry],
        )

    @pl.loop(0, requests * per_request)
    def _(entry):
        fetch(entry).start()

    lane = lax.broadcasted_iota(jnp.int32, (CK, 128), 1)
    triangle = lax.broadcasted_iota(jnp.int32, (TQ, TQ), 1) <= lax.broadcasted_iota(
        jnp.int32, (TQ, TQ), 0
    )
    column = lax.broadcasted_iota(jnp.int32, (TQ, CK), 1)

    def with_ones(kv):
        return jnp.where(lane[: kv.shape[0]] < HD, jnp.ones_like(kv), kv)

    def scores_of(queries, kv):
        return lax.dot_general(queries, kv, CONTRACT, preferred_element_type=jnp.float32)

    def mix(weights, kv):
        return jnp.dot(weights.astype(jnp.bfloat16), with_ones(kv), preferred_element_type=jnp.float32)

    @pl.loop(0, requests)
    def _(request):
        base = pl.multiple_of(request * span, span)
        length = lengths[request]

        for tile in range(tiles):
            queries = q_ref[pl.ds(base + tile * TQ, TQ), :]
            own = kv_ref[pl.ds(base + tile * TQ, TQ), :]
            diagonal = jnp.where(triangle, scores_of(queries, own), NEGATIVE)
            high = jnp.max(diagonal, axis=1, keepdims=True)
            earlier = []
            for at in range(tile):
                block = kv_ref[pl.ds(base + at * TQ, TQ), :]
                scores = scores_of(queries, block)
                high = jnp.maximum(high, jnp.max(scores, axis=1, keepdims=True))
                earlier.append((block, scores))
            result = mix(jnp.exp(diagonal - high), own)
            for block, scores in earlier:
                result = result + mix(jnp.exp(scores - high), block)
            total[pl.ds(tile * TQ, TQ), :] = result
            top[pl.ds(tile * TQ, TQ), :] = jnp.broadcast_to(high, (TQ, 128))

        @pl.loop(0, per_request)
        def _(page):
            fetch(request * per_request + page).wait()

        def chunk(index, masked):
            first = pl.multiple_of(index * CK, CK)
            kv = pages[request, pl.ds(first, CK), :]
            values = with_ones(kv)
            for tile in range(tiles):
                rows = pl.ds(tile * TQ, TQ)
                scores = scores_of(q_ref[pl.ds(base + tile * TQ, TQ), :], kv)
                if masked:
                    scores = jnp.where(column < length - first, scores, NEGATIVE)
                old = top[rows, :]
                new = jnp.maximum(old, jnp.max(scores, axis=1, keepdims=True))
                weights = jnp.exp(scores - new[:, :1]).astype(jnp.bfloat16)
                total[rows, :] = total[rows, :] * jnp.exp(old - new) + jnp.dot(
                    weights, values, preferred_element_type=jnp.float32
                )
                top[rows, :] = new

        whole = length // CK

        @pl.loop(0, whole)
        def _(index):
            chunk(index, False)

        @pl.when(length % CK > 0)
        def _():
            chunk(whole, True)

        for tile in range(tiles):
            low = total[pl.ds(tile * TQ, TQ // 2), :]
            high = total[pl.ds(tile * TQ + TQ // 2, TQ // 2), :]
            side = lax.broadcasted_iota(jnp.int32, low.shape, 1) < HD
            low_out = pltpu.roll(low, HD, 1) / low
            high_out = high / pltpu.roll(high, HD, 1)
            out_ref[request * tiles + tile] = jnp.where(side, low_out, high_out).astype(jnp.bfloat16)


def attention(table, lengths, queries, kv, cache):
    rows = queries.shape[0]
    requests = lengths.shape[0]
    cached = table.shape[0] // requests * PAGE
    vmem = pl.BlockSpec(memory_space=pltpu.VMEM)
    smem = pl.BlockSpec(memory_space=pltpu.SMEM)
    return pl.pallas_call(
        attention_kernel,
        out_shape=jax.ShapeDtypeStruct((rows // TQ, TQ // 2, 2 * HD), jnp.bfloat16),
        in_specs=[smem, smem, vmem, vmem, pl.BlockSpec(memory_space=pl.ANY)],
        out_specs=vmem,
        scratch_shapes=[
            pltpu.VMEM((requests, cached, 2 * HD), jnp.bfloat16),
            pltpu.VMEM((rows // requests, 128), jnp.float32),
            pltpu.VMEM((rows // requests, 2 * HD), jnp.float32),
            pltpu.SemaphoreType.DMA((table.shape[0],)),
        ],
        cost_estimate=pl.CostEstimate(
            flops=4 * rows * 128 * 2560, bytes_accessed=8 << 20, transcendentals=rows * 2560
        ),
        compiler_params=pltpu.CompilerParams(vmem_limit_bytes=40 << 20),
        name="paged_attention",
    )(table, lengths, queries, kv, cache)


def body(
    tokens,
    gain_attn,
    w_qkv,
    w_attn_out,
    kv_cache,
    page_table,
    cached_lengths,
    gain_moe,
    w_router,
    routes,
    w_in,
    w_out,
):
    normed = rms_norm(tokens, gain_attn).astype(jnp.bfloat16)
    zeros = jnp.zeros((w_qkv.shape[0], HD), w_qkv.dtype)
    packed = jnp.concatenate([w_qkv[:, :HD] * 0.125, zeros, w_qkv[:, HD:]], axis=1)
    full_qkv = lax.all_gather(packed, "batch", axis=0, tiled=True)
    projected = jnp.dot(
        lax.all_gather(normed, "tensor", axis=0, tiled=True),
        full_qkv,
        preferred_element_type=jnp.float32,
    ).astype(jnp.bfloat16)
    out_weights = lax.all_gather(w_attn_out, ("batch", "tensor"), axis=0)
    lanes = lax.axis_size("tensor")
    out_weights = out_weights.reshape(-1, lanes, *w_attn_out.shape)
    rows_here = tokens.shape[0]
    attended = attention(
        page_table[0], cached_lengths, projected[:, : 2 * HD], projected[:, 2 * HD :], kv_cache
    )
    shares = lax.all_to_all(attended, "tensor", split_axis=0, concat_axis=0, tiled=True)
    shares = shares.reshape(lanes, TQ // 2, 2, HD).transpose(2, 1, 0, 3).reshape(rows_here, lanes * HD)
    out_weights = out_weights.transpose(0, 2, 1, 3).reshape(-1, lanes * HD)
    projection = lax.dot_general(shares, out_weights, CONTRACT, preferred_element_type=jnp.float32)
    state = tokens.astype(jnp.float32) + projection
    normed_moe = rms_norm(state, gain_moe).astype(jnp.bfloat16)
    logits = jnp.dot(normed_moe, w_router, preferred_element_type=jnp.float32)
    experts = w_router.shape[1]
    top_count = routes.shape[1]
    onehot = (routes[:, :, None] == jnp.arange(experts, dtype=jnp.int32)[None, None, :]).astype(
        jnp.int32
    )
    picked = jnp.sum(onehot.astype(jnp.float32) * logits[:, None, :], axis=2)
    squashed = jax.nn.sigmoid(picked)
    gates = squashed / jnp.sum(squashed, axis=1, keepdims=True)
    flat_hits = onehot.reshape(rows_here * top_count, experts)
    before = jnp.cumsum(flat_hits, axis=0) - flat_hits
    slots = jnp.sum(before * flat_hits, axis=1).reshape(rows_here, top_count)
    capacity = max(2, (5 * rows_here * top_count + 4 * experts - 1) // (4 * experts))
    position = routes * capacity + slots
    slot_ids = jnp.arange(experts * capacity, dtype=jnp.int32)
    placing = jnp.any(slot_ids[:, None, None] == position[None, :, :], axis=2).astype(jnp.bfloat16)
    buffer = jnp.dot(placing, normed_moe, preferred_element_type=jnp.float32).astype(jnp.bfloat16)
    buffer = buffer.reshape(lanes, w_in.shape[0], capacity, normed_moe.shape[1])
    width_ff = w_out.shape[1]
    inner = jnp.einsum(
        "sekd,edf->sekf",
        lax.all_to_all(buffer, "tensor", split_axis=0, concat_axis=0, tiled=True),
        w_in,
        preferred_element_type=jnp.float32,
    )
    active = (jax.nn.gelu(inner[..., :width_ff], approximate=True) * inner[..., width_ff:]).astype(
        jnp.bfloat16
    )
    results = jnp.einsum(
        "sekf,efd->sekd", active, w_out, preferred_element_type=jnp.float32
    ).astype(jnp.bfloat16)
    returned = lax.all_to_all(results, "tensor", split_axis=0, concat_axis=0, tiled=True).reshape(
        experts * capacity, normed_moe.shape[1]
    )
    mixed = state
    for rank in range(top_count):
        pick = (position[:, rank : rank + 1] == slot_ids[None, :]).astype(jnp.bfloat16)
        mixed = mixed + gates[:, rank : rank + 1] * jnp.dot(
            pick, returned, preferred_element_type=jnp.float32
        )
    return mixed.astype(jnp.bfloat16)


def solution(mesh):
    in_specs = (
        P(("batch", "tensor"), None),
        P(),
        P("batch", "tensor"),
        P("batch", "tensor"),
        P("batch", None, "tensor"),
        P("batch", None),
        P("batch"),
        P(),
        P(),
        P(("batch", "tensor"), None),
        P("tensor", None, None),
        P("tensor", None, None),
    )
    out_specs = P(("batch", "tensor"), None)
    return jax.shard_map(body, mesh=mesh, in_specs=in_specs, out_specs=out_specs, check_vma=False)
```

```python
import math

import jax
import jax.numpy as jnp
from jax import lax
from jax.experimental import pallas as pl
from jax.experimental.pallas import tpu as pltpu
from jax.sharding import PartitionSpec as P

HD = 64


EPSILON = 1e-06
NEGATIVE = -1e30
CONTRACT = (((1,), (1,)), ((), ()))


def rms_norm(values, gain):
    values = values.astype(jnp.float32)
    mean_square = jnp.mean(values * values, axis=-1, keepdims=True)
    return values * lax.rsqrt(mean_square + EPSILON) * gain


PAGE = 128
TQ = 256
CK = 512


def attention_kernel(
    table, lengths, blocks_ref, cache_ref, out_ref, pages, q_ref, top, total, sems
):
    requests, per_request = pages.shape[0], pages.shape[1] // PAGE
    tiles = blocks_ref.shape[0] // requests
    half = TQ // 2

    def fetch(entry):
        return pltpu.make_async_copy(
            cache_ref.at[table[entry]],
            pages.at[entry // per_request, pl.ds((entry % per_request) * PAGE, PAGE), :],
            sems.at[entry],
        )

    @pl.loop(0, requests * per_request)
    def _(entry):
        fetch(entry).start()

    lane = lax.broadcasted_iota(jnp.int32, (CK, 128), 1)
    triangle = lax.broadcasted_iota(jnp.int32, (TQ, TQ), 1) <= lax.broadcasted_iota(
        jnp.int32, (TQ, TQ), 0
    )
    column = lax.broadcasted_iota(jnp.int32, (TQ, CK), 1)

    def with_ones(kv):
        return jnp.where(lane[: kv.shape[0]] < HD, jnp.ones_like(kv), kv)

    def scores_of(queries, kv):
        return lax.dot_general(queries, kv, CONTRACT, preferred_element_type=jnp.float32)

    def mix(weights, kv):
        return jnp.dot(weights.astype(jnp.bfloat16), with_ones(kv), preferred_element_type=jnp.float32)

    @pl.loop(0, requests)
    def _(request):
        length = lengths[request]
        left = lax.broadcasted_iota(jnp.int32, (half, 2 * HD), 1) < HD
        for tile in range(tiles):
            both = blocks_ref[request * tiles + tile, pl.ds(0, half), :].astype(jnp.float32)
            for part, queries in enumerate((both, pltpu.roll(both, HD, 1))):
                q_ref[pl.ds(tile * TQ + part * half, half), :] = jnp.where(
                    left, queries, 0.0
                ).astype(jnp.bfloat16)

        for tile in range(tiles):
            queries = q_ref[pl.ds(tile * TQ, TQ), :]
            own = blocks_ref[request * tiles + tile, pl.ds(half, TQ), :]
            diagonal = jnp.where(triangle, scores_of(queries, own), NEGATIVE)
            high = jnp.max(diagonal, axis=1, keepdims=True)
            earlier = []
            for at in range(tile):
                block = blocks_ref[request * tiles + at, pl.ds(half, TQ), :]
                scores = scores_of(queries, block)
                high = jnp.maximum(high, jnp.max(scores, axis=1, keepdims=True))
                earlier.append((block, scores))
            result = mix(jnp.exp(diagonal - high), own)
            for block, scores in earlier:
                result = result + mix(jnp.exp(scores - high), block)
            total[pl.ds(tile * TQ, TQ), :] = result
            top[pl.ds(tile * TQ, TQ), :] = jnp.broadcast_to(high, (TQ, 128))

        @pl.loop(0, per_request)
        def _(page):
            fetch(request * per_request + page).wait()

        def chunk(index, masked):
            first = pl.multiple_of(index * CK, CK)
            kv = pages[request, pl.ds(first, CK), :]
            values = with_ones(kv)
            for tile in range(tiles):
                rows = pl.ds(tile * TQ, TQ)
                scores = scores_of(q_ref[rows, :], kv)
                if masked:
                    scores = jnp.where(column < length - first, scores, NEGATIVE)
                old = top[rows, :]
                new = jnp.maximum(old, jnp.max(scores, axis=1, keepdims=True))
                weights = jnp.exp(scores - new[:, :1]).astype(jnp.bfloat16)
                total[rows, :] = total[rows, :] * jnp.exp(old - new) + jnp.dot(
                    weights, values, preferred_element_type=jnp.float32
                )
                top[rows, :] = new

        whole = length // CK

        @pl.loop(0, whole)
        def _(index):
            chunk(index, False)

        @pl.when(length % CK > 0)
        def _():
            chunk(whole, True)

        for tile in range(tiles):
            low = total[pl.ds(tile * TQ, TQ // 2), :]
            high = total[pl.ds(tile * TQ + TQ // 2, TQ // 2), :]
            side = lax.broadcasted_iota(jnp.int32, low.shape, 1) < HD
            low_out = pltpu.roll(low, HD, 1) / low
            high_out = high / pltpu.roll(high, HD, 1)
            out_ref[request * tiles + tile] = jnp.where(side, low_out, high_out).astype(jnp.bfloat16)


def attention(table, lengths, blocks, cache):
    rows = blocks.shape[0] * TQ
    requests = lengths.shape[0]
    cached = table.shape[0] // requests * PAGE
    vmem = pl.BlockSpec(memory_space=pltpu.VMEM)
    smem = pl.BlockSpec(memory_space=pltpu.SMEM)
    return pl.pallas_call(
        attention_kernel,
        out_shape=jax.ShapeDtypeStruct((rows // TQ, TQ // 2, 2 * HD), jnp.bfloat16),
        in_specs=[smem, smem, vmem, pl.BlockSpec(memory_space=pl.ANY)],
        out_specs=vmem,
        scratch_shapes=[
            pltpu.VMEM((requests, cached, 2 * HD), jnp.bfloat16),
            pltpu.VMEM((rows // requests, 2 * HD), jnp.bfloat16),
            pltpu.VMEM((rows // requests, 128), jnp.float32),
            pltpu.VMEM((rows // requests, 2 * HD), jnp.float32),
            pltpu.SemaphoreType.DMA((table.shape[0],)),
        ],
        cost_estimate=pl.CostEstimate(
            flops=4 * rows * 128 * 2560, bytes_accessed=8 << 20, transcendentals=rows * 2560
        ),
        compiler_params=pltpu.CompilerParams(vmem_limit_bytes=40 << 20),
        name="paged_attention",
    )(table, lengths, blocks, cache)


MESH = pl.DeviceIdType.MESH
SIDE = 4


def place():
    batch, tensor = lax.axis_index("batch"), lax.axis_index("tensor")
    return batch // 2, batch % 2, tensor // SIDE, tensor % SIDE


def device(y, core, z, x):
    return {"batch": (y % SIDE) * 2 + core % 2, "tensor": (z % SIDE) * SIDE + x % SIDE}


def send(source, target, sems, at, to):
    return pltpu.make_async_remote_copy(
        src_ref=source,
        dst_ref=target,
        send_sem=sems.at[0, at],
        recv_sem=sems.at[1, at],
        device_id=to,
        device_id_type=MESH,
    )


def project_kernel(
    x_ref, gain_ref, w_ref, out_ref, others, shards, w_query, w_kv, normed, packs,
    w_sems, core_sems, x_sems, z_sems, local_sems,
):
    y, core, z, x = place()
    half = TQ // 2
    around = [(dy, dz) for dy in range(SIDE) for dz in range(SIDE) if dy or dz]
    partner = device(y, core + 1, z, x)
    right, left = device(y, core, z, x + 1), device(y, core, z, x + SIDE - 1)

    barrier = pltpu.get_barrier_semaphore()
    peers = [device(y + dy, core, z + dz, x) for dy, dz in around] + [partner, right, left]
    for peer in peers:
        pl.semaphore_signal(barrier, inc=1, device_id=peer, device_id_type=MESH)
    pl.semaphore_wait(barrier, len(peers))

    w_copies = {}
    for at, (dy, dz) in enumerate(around):
        w_copies[dy, dz] = send(
            w_ref, shards.at[core, y, z], w_sems, at, device(y + dy, core, z + dz, x)
        )
        w_copies[dy, dz].start()
    first, second = pl.ds(0, half), pl.ds(half, half)
    x_copies = [
        send(x_ref.at[first], others.at[0, first], x_sems, 0, right),
        send(x_ref.at[second], others.at[1, second], x_sems, 1, left),
        send(x_ref.at[second], others.at[0, second], x_sems, 2, right),
        send(x_ref.at[first], others.at[1, first], x_sems, 3, left),
        send(others.at[0, first], others.at[2, first], x_sems, 4, right),
        send(others.at[1, second], others.at[2, second], x_sems, 5, left),
    ]
    for copy in x_copies[:4]:
        copy.start()
    own = pltpu.make_async_copy(w_ref, shards.at[core, y, z], local_sems.at[0])
    own.start()

    def norm(values):
        values = values.astype(jnp.float32)
        mean_square = jnp.mean(values * values, axis=-1, keepdims=True)
        normed[...] = (values * lax.rsqrt(mean_square + EPSILON) * gain_ref[...]).astype(jnp.bfloat16)

    norm(x_ref[...])
    own.wait()
    core_copies = []
    for dy in range(SIDE):
        for dz in range(SIDE):
            if dy or dz:
                w_copies[dy, dz].wait_recv()
        source = (y - dy + SIDE) % SIDE
        copy = send(shards.at[core, source], shards.at[core, source], core_sems, dy, partner)
        copy.start()
        core_copies.append(copy)
        if dy == 1:
            x_copies[0].wait_recv()
            x_copies[4].start()
            x_copies[1].wait_recv()
            x_copies[5].start()
    for copy in core_copies:
        copy.wait_recv()
    for index in range(2 * SIDE):
        lanes = pl.ds(index * 128, 128)
        for head in range(SIDE):
            w_query[pl.ds(head * HD, HD), lanes] = shards[index % 2, index // 2, head, pl.ds(0, HD), :]
            w_kv[pl.ds(head * 2 * HD, 2 * HD), lanes] = shards[
                index % 2, index // 2, head, pl.ds(HD, 2 * HD), :
            ]

    side = lax.broadcasted_iota(jnp.int32, (half, 2 * HD), 1) < HD
    z_copies = []
    for step, shift in enumerate((0, SIDE - 1, 1, 2)):
        if step == 1:
            x_copies[2].wait_recv()
        if step == 2:
            x_copies[3].wait_recv()
        if step == 3:
            x_copies[4].wait_recv()
            x_copies[5].wait_recv()
        if step:
            norm(others[step - 1])
        queries = lax.dot_general(
            normed[...], w_query[...], CONTRACT, preferred_element_type=jnp.float32
        ) * (1.0 / math.sqrt(HD))
        kv = lax.dot_general(
            normed[...], w_kv[...], CONTRACT, preferred_element_type=jnp.float32
        ).astype(jnp.bfloat16)
        for pair in range(SIDE // 2):
            early = queries[:half, pair * 2 * HD : (pair + 1) * 2 * HD]
            late = queries[half:, pair * 2 * HD : (pair + 1) * 2 * HD]
            packs[step, 2 * pair, first, :] = jnp.where(
                side, early, pltpu.roll(late, HD, 1)
            ).astype(jnp.bfloat16)
            packs[step, 2 * pair + 1, first, :] = jnp.where(
                side, pltpu.roll(early, HD, 1), late
            ).astype(jnp.bfloat16)
        for head in range(SIDE):
            packs[step, head, pl.ds(half, TQ), :] = kv[:, head * 2 * HD : (head + 1) * 2 * HD]
        block = out_ref.at[z * SIDE + (x + shift) % SIDE]
        for dz in (2, 1, 3):
            copy = send(
                packs.at[step, (z + dz) % SIDE], block, z_sems, step * 3 + dz - 1,
                device(y, core, z + dz, x),
            )
            copy.start()
            z_copies.append(copy)
        copy = pltpu.make_async_copy(packs.at[step, z], block, local_sems.at[1 + step])
        copy.start()
        z_copies.append(copy)
    for copy in z_copies:
        copy.wait()
    for copy in list(w_copies.values()) + x_copies + core_copies:
        copy.wait_send()


def project(tokens, gain, weights):
    rows, width = tokens.shape
    vmem = pl.BlockSpec(memory_space=pltpu.VMEM)
    bf16 = jnp.bfloat16
    return pl.pallas_call(
        project_kernel,
        out_shape=jax.ShapeDtypeStruct((SIDE * SIDE, 3 * TQ // 2, 2 * HD), bf16),
        in_specs=[vmem] * 3,
        out_specs=vmem,
        scratch_shapes=[
            pltpu.VMEM((3, rows, width), bf16),
            pltpu.VMEM((2, SIDE, SIDE, *weights.shape), bf16),
            pltpu.VMEM((SIDE * HD, width), bf16),
            pltpu.VMEM((SIDE * 2 * HD, width), bf16),
            pltpu.VMEM((rows, width), bf16),
            pltpu.VMEM((SIDE, SIDE, 3 * TQ // 2, 2 * HD), bf16),
            pltpu.SemaphoreType.DMA((2, 15)),
            pltpu.SemaphoreType.DMA((2, SIDE)),
            pltpu.SemaphoreType.DMA((2, 6)),
            pltpu.SemaphoreType.DMA((2, 12)),
            pltpu.SemaphoreType.DMA((1 + SIDE,)),
        ],
        cost_estimate=pl.CostEstimate(
            flops=6 * SIDE * rows * width * HD * SIDE, bytes_accessed=8 << 20, transcendentals=0
        ),
        compiler_params=pltpu.CompilerParams(
            collective_id=0, has_side_effects=True, vmem_limit_bytes=32 << 20
        ),
        name="gather_project",
    )(tokens, gain, weights)


def body(
    tokens,
    gain_attn,
    w_qkv,
    w_attn_out,
    kv_cache,
    page_table,
    cached_lengths,
    gain_moe,
    w_router,
    routes,
    w_in,
    w_out,
):
    lanes = lax.axis_size("tensor")
    rows_here = tokens.shape[0]
    out_weights = lax.all_gather(w_attn_out.T, ("batch", "tensor"), axis=0)
    out_weights = out_weights.reshape(-1, lanes * HD, w_attn_out.shape[0])
    blocks = project(tokens, gain_attn.reshape(1, -1), w_qkv.T)
    attended = attention(page_table[0], cached_lengths, blocks, kv_cache)
    shares = lax.all_to_all(attended, "tensor", split_axis=0, concat_axis=0, tiled=True)
    shares = shares.reshape(lanes, TQ // 2, 2, HD).transpose(2, 1, 0, 3).reshape(rows_here, lanes * HD)
    projection = jnp.einsum(
        "tk,bkn->tbn", shares, out_weights, preferred_element_type=jnp.float32
    ).reshape(rows_here, -1)
    state = tokens.astype(jnp.float32) + projection
    normed_moe = rms_norm(state, gain_moe).astype(jnp.bfloat16)
    logits = jnp.dot(normed_moe, w_router, preferred_element_type=jnp.float32)
    experts = w_router.shape[1]
    top_count = routes.shape[1]
    onehot = (routes[:, :, None] == jnp.arange(experts, dtype=jnp.int32)[None, None, :]).astype(
        jnp.int32
    )
    picked = jnp.sum(onehot.astype(jnp.float32) * logits[:, None, :], axis=2)
    squashed = jax.nn.sigmoid(picked)
    gates = squashed / jnp.sum(squashed, axis=1, keepdims=True)
    flat_hits = onehot.reshape(rows_here * top_count, experts)
    before = jnp.cumsum(flat_hits, axis=0) - flat_hits
    slots = jnp.sum(before * flat_hits, axis=1).reshape(rows_here, top_count)
    capacity = max(2, (5 * rows_here * top_count + 4 * experts - 1) // (4 * experts))
    position = routes * capacity + slots
    slot_ids = jnp.arange(experts * capacity, dtype=jnp.int32)
    placing = jnp.any(slot_ids[:, None, None] == position[None, :, :], axis=2).astype(jnp.bfloat16)
    buffer = jnp.dot(placing, normed_moe, preferred_element_type=jnp.float32).astype(jnp.bfloat16)
    buffer = buffer.reshape(lanes, w_in.shape[0], capacity, normed_moe.shape[1])
    width_ff = w_out.shape[1]
    inner = jnp.einsum(
        "sekd,edf->sekf",
        lax.all_to_all(buffer, "tensor", split_axis=0, concat_axis=0, tiled=True),
        w_in,
        preferred_element_type=jnp.float32,
    )
    active = (jax.nn.gelu(inner[..., :width_ff], approximate=True) * inner[..., width_ff:]).astype(
        jnp.bfloat16
    )
    results = jnp.einsum(
        "sekf,efd->sekd", active, w_out, preferred_element_type=jnp.float32
    ).astype(jnp.bfloat16)
    returned = lax.all_to_all(results, "tensor", split_axis=0, concat_axis=0, tiled=True).reshape(
        experts * capacity, normed_moe.shape[1]
    )
    mixed = state
    for rank in range(top_count):
        pick = (position[:, rank : rank + 1] == slot_ids[None, :]).astype(jnp.bfloat16)
        mixed = mixed + gates[:, rank : rank + 1] * jnp.dot(
            pick, returned, preferred_element_type=jnp.float32
        )
    return mixed.astype(jnp.bfloat16)


def solution(mesh):
    in_specs = (
        P(("batch", "tensor"), None),
        P(),
        P("batch", "tensor"),
        P("batch", "tensor"),
        P("batch", None, "tensor"),
        P("batch", None),
        P("batch"),
        P(),
        P(),
        P(("batch", "tensor"), None),
        P("tensor", None, None),
        P("tensor", None, None),
    )
    out_specs = P(("batch", "tensor"), None)
    return jax.shard_map(body, mesh=mesh, in_specs=in_specs, out_specs=out_specs, check_vma=False)
```

```python
import math

import jax
import jax.numpy as jnp
from jax import lax
from jax.experimental import pallas as pl
from jax.experimental.pallas import tpu as pltpu
from jax.sharding import PartitionSpec as P

HD = 64


EPSILON = 1e-06
NEGATIVE = -1e30
CONTRACT = (((1,), (1,)), ((), ()))


def rms_norm(values, gain):
    values = values.astype(jnp.float32)
    mean_square = jnp.mean(values * values, axis=-1, keepdims=True)
    return values * lax.rsqrt(mean_square + EPSILON) * gain


PAGE = 128
TQ = 256
CK = 512


def attention_kernel(table, lengths, blocks_ref, cache_ref, out_ref, q_ref, kv_ref, flipped, top, total):
    requests = lengths.shape[0]
    tiles = blocks_ref.shape[0] // requests
    per_request = table.shape[0] // requests
    half = TQ // 2
    left = lax.broadcasted_iota(jnp.int32, (half, 2 * HD), 1) < HD
    triangle = lax.broadcasted_iota(jnp.int32, (TQ, TQ), 0) <= lax.broadcasted_iota(
        jnp.int32, (TQ, TQ), 1
    )
    line = lax.broadcasted_iota(jnp.int32, (CK, TQ), 0)
    flipped[pl.ds(HD, 16), :] = jnp.ones((16, flipped.shape[1]), jnp.bfloat16)

    def scores_of(kv, tile):
        return lax.dot_general(
            kv, q_ref[pl.ds(tile * TQ, TQ), :], CONTRACT, preferred_element_type=jnp.float32
        )

    @pl.loop(0, requests)
    def _(request):
        length = lengths[request]
        for tile in range(tiles):
            block = blocks_ref[request * tiles + tile]
            both = block[:half].astype(jnp.float32)
            for part, queries in enumerate((both, pltpu.roll(both, HD, 1))):
                q_ref[pl.ds(tile * TQ + part * half, half), :] = jnp.where(
                    left, queries, 0.0
                ).astype(jnp.bfloat16)
            kv = block[half:]
            kv_ref[pl.ds(tile * TQ, TQ), :] = kv
            flipped[pl.ds(0, HD), pl.ds(tile * TQ, TQ)] = kv.T[HD:]

        def start(tile):
            earlier = scores_of(kv_ref[pl.ds(0, tile * TQ), :], tile) if tile else None
            return earlier, scores_of(kv_ref[pl.ds(tile * TQ, TQ), :], tile)

        ahead = start(0)
        for tile in range(tiles):
            earlier, diagonal = ahead
            if tile + 1 < tiles:
                ahead = start(tile + 1)
            columns = pl.ds(tile * TQ, TQ)
            diagonal = jnp.where(triangle, diagonal, NEGATIVE)
            high = jnp.max(diagonal, axis=0, keepdims=True)
            if tile:
                high = jnp.maximum(high, jnp.max(earlier, axis=0, keepdims=True))
            result = jnp.dot(
                flipped[:, columns],
                jnp.exp(diagonal - high).astype(jnp.bfloat16),
                preferred_element_type=jnp.float32,
            )
            if tile:
                result = result + jnp.dot(
                    flipped[:, pl.ds(0, tile * TQ)],
                    jnp.exp(earlier - high).astype(jnp.bfloat16),
                    preferred_element_type=jnp.float32,
                )
            total[:, columns] = result
            top[:, columns] = high

        def chunk(index, masked):
            pages = [
                cache_ref[table[request * per_request + index * (CK // PAGE) + at]]
                for at in range(CK // PAGE)
            ]
            kv = jnp.concatenate(pages, axis=0)
            values = jnp.concatenate([kv.T[HD:], jnp.ones((16, CK), jnp.bfloat16)], axis=0)
            ahead = scores_of(kv, 0)
            for tile in range(tiles):
                scores = ahead
                if tile + 1 < tiles:
                    ahead = scores_of(kv, tile + 1)
                columns = pl.ds(tile * TQ, TQ)
                if masked:
                    scores = jnp.where(line < length - index * CK, scores, NEGATIVE)
                old = top[:, columns]
                new = jnp.maximum(old, jnp.max(scores, axis=0, keepdims=True))
                weights = jnp.exp(scores - new).astype(jnp.bfloat16)
                total[:, columns] = total[:, columns] * jnp.exp(old - new) + jnp.dot(
                    values, weights, preferred_element_type=jnp.float32
                )
                top[:, columns] = new

        whole = length // CK

        @pl.loop(0, whole)
        def _(index):
            chunk(index, False)

        @pl.when(length % CK > 0)
        def _():
            chunk(whole, True)

        for tile in range(tiles):
            columns = pl.ds(tile * TQ, TQ)
            ratio = total[pl.ds(0, HD), columns] / total[pl.ds(HD, 1), columns]
            ratio = jnp.concatenate([ratio[:, :half], ratio[:, half:]], axis=0)
            out_ref[request * tiles + tile] = ratio.T.astype(jnp.bfloat16)


def attention(table, lengths, blocks, cache):
    rows = blocks.shape[0] * TQ
    requests = lengths.shape[0]
    span = rows // requests
    vmem = pl.BlockSpec(memory_space=pltpu.VMEM)
    smem = pl.BlockSpec(memory_space=pltpu.SMEM)
    return pl.pallas_call(
        attention_kernel,
        out_shape=jax.ShapeDtypeStruct((rows // TQ, TQ // 2, 2 * HD), jnp.bfloat16),
        in_specs=[smem, smem, vmem, vmem],
        out_specs=vmem,
        scratch_shapes=[
            pltpu.VMEM((span, 2 * HD), jnp.bfloat16),
            pltpu.VMEM((span, 2 * HD), jnp.bfloat16),
            pltpu.VMEM((HD + 16, span), jnp.bfloat16),
            pltpu.VMEM((1, span), jnp.float32),
            pltpu.VMEM((HD + 16, span), jnp.float32),
        ],
        cost_estimate=pl.CostEstimate(
            flops=4 * rows * 128 * 2560, bytes_accessed=8 << 20, transcendentals=rows * 2560
        ),
        compiler_params=pltpu.CompilerParams(vmem_limit_bytes=24 << 20),
        name="paged_attention",
    )(table, lengths, blocks, cache)


MESH = pl.DeviceIdType.MESH
SIDE = 4


def place():
    batch, tensor = lax.axis_index("batch"), lax.axis_index("tensor")
    return batch // 2, batch % 2, tensor // SIDE, tensor % SIDE


def device(y, core, z, x):
    return {"batch": (y % SIDE) * 2 + core % 2, "tensor": (z % SIDE) * SIDE + x % SIDE}


def send(source, target, sems, at, to):
    return pltpu.make_async_remote_copy(
        src_ref=source,
        dst_ref=target,
        send_sem=sems.at[0, at],
        recv_sem=sems.at[1, at],
        device_id=to,
        device_id_type=MESH,
    )


def project_kernel(
    x_ref, gain_ref, w_ref, out_ref, others, shards, w_query, w_kv, normed, packs,
    w_sems, core_sems, x_sems, z_sems, local_sems,
):
    y, core, z, x = place()
    half = TQ // 2
    around = [(dy, dz) for dy in range(SIDE) for dz in range(SIDE) if dy or dz]
    partner = device(y, core + 1, z, x)
    right, left = device(y, core, z, x + 1), device(y, core, z, x + SIDE - 1)

    barrier = pltpu.get_barrier_semaphore()
    peers = [device(y + dy, core, z + dz, x) for dy, dz in around] + [partner, right, left]
    for peer in peers:
        pl.semaphore_signal(barrier, inc=1, device_id=peer, device_id_type=MESH)
    pl.semaphore_wait(barrier, len(peers))

    w_copies = {}
    for at, (dy, dz) in enumerate(around):
        w_copies[dy, dz] = send(
            w_ref, shards.at[core, y, z], w_sems, at, device(y + dy, core, z + dz, x)
        )
        w_copies[dy, dz].start()
    first, second = pl.ds(0, half), pl.ds(half, half)
    x_copies = [
        send(x_ref.at[first], others.at[0, first], x_sems, 0, right),
        send(x_ref.at[second], others.at[1, second], x_sems, 1, left),
        send(x_ref.at[second], others.at[0, second], x_sems, 2, right),
        send(x_ref.at[first], others.at[1, first], x_sems, 3, left),
        send(others.at[0, first], others.at[2, first], x_sems, 4, right),
        send(others.at[1, second], others.at[2, second], x_sems, 5, left),
    ]
    for copy in x_copies[:4]:
        copy.start()
    own = pltpu.make_async_copy(w_ref, shards.at[core, y, z], local_sems.at[0])
    own.start()

    def norm(values):
        values = values.astype(jnp.float32)
        mean_square = jnp.mean(values * values, axis=-1, keepdims=True)
        normed[...] = (values * lax.rsqrt(mean_square + EPSILON) * gain_ref[...]).astype(jnp.bfloat16)

    norm(x_ref[...])
    own.wait()
    core_copies = []
    for dy in range(SIDE):
        for dz in range(SIDE):
            if dy or dz:
                w_copies[dy, dz].wait_recv()
        source = (y - dy + SIDE) % SIDE
        copy = send(shards.at[core, source], shards.at[core, source], core_sems, dy, partner)
        copy.start()
        core_copies.append(copy)
        if dy == 1:
            x_copies[0].wait_recv()
            x_copies[4].start()
            x_copies[1].wait_recv()
            x_copies[5].start()
    for copy in core_copies:
        copy.wait_recv()
    for index in range(2 * SIDE):
        lanes = pl.ds(index * 128, 128)
        for head in range(SIDE):
            w_query[pl.ds(head * HD, HD), lanes] = shards[index % 2, index // 2, head, pl.ds(0, HD), :]
            w_kv[pl.ds(head * 2 * HD, 2 * HD), lanes] = shards[
                index % 2, index // 2, head, pl.ds(HD, 2 * HD), :
            ]

    side = lax.broadcasted_iota(jnp.int32, (half, 2 * HD), 1) < HD
    z_copies = []
    for step, shift in enumerate((0, SIDE - 1, 1, 2)):
        if step == 1:
            x_copies[2].wait_recv()
        if step == 2:
            x_copies[3].wait_recv()
        if step == 3:
            x_copies[4].wait_recv()
            x_copies[5].wait_recv()
        if step:
            norm(others[step - 1])
        queries = lax.dot_general(
            normed[...], w_query[...], CONTRACT, preferred_element_type=jnp.float32
        ) * (1.0 / math.sqrt(HD))
        kv = lax.dot_general(
            normed[...], w_kv[...], CONTRACT, preferred_element_type=jnp.float32
        ).astype(jnp.bfloat16)
        for pair in range(SIDE // 2):
            early = queries[:half, pair * 2 * HD : (pair + 1) * 2 * HD]
            late = queries[half:, pair * 2 * HD : (pair + 1) * 2 * HD]
            packs[step, 2 * pair, first, :] = jnp.where(
                side, early, pltpu.roll(late, HD, 1)
            ).astype(jnp.bfloat16)
            packs[step, 2 * pair + 1, first, :] = jnp.where(
                side, pltpu.roll(early, HD, 1), late
            ).astype(jnp.bfloat16)
        for head in range(SIDE):
            packs[step, head, pl.ds(half, TQ), :] = kv[:, head * 2 * HD : (head + 1) * 2 * HD]
        block = out_ref.at[z * SIDE + (x + shift) % SIDE]
        for dz in (2, 1, 3):
            copy = send(
                packs.at[step, (z + dz) % SIDE], block, z_sems, step * 3 + dz - 1,
                device(y, core, z + dz, x),
            )
            copy.start()
            z_copies.append(copy)
        copy = pltpu.make_async_copy(packs.at[step, z], block, local_sems.at[1 + step])
        copy.start()
        z_copies.append(copy)
    for copy in z_copies:
        copy.wait()
    for copy in list(w_copies.values()) + x_copies + core_copies:
        copy.wait_send()


def project(tokens, gain, weights):
    rows, width = tokens.shape
    vmem = pl.BlockSpec(memory_space=pltpu.VMEM)
    bf16 = jnp.bfloat16
    return pl.pallas_call(
        project_kernel,
        out_shape=jax.ShapeDtypeStruct((SIDE * SIDE, 3 * TQ // 2, 2 * HD), bf16),
        in_specs=[vmem] * 3,
        out_specs=vmem,
        scratch_shapes=[
            pltpu.VMEM((3, rows, width), bf16),
            pltpu.VMEM((2, SIDE, SIDE, *weights.shape), bf16),
            pltpu.VMEM((SIDE * HD, width), bf16),
            pltpu.VMEM((SIDE * 2 * HD, width), bf16),
            pltpu.VMEM((rows, width), bf16),
            pltpu.VMEM((SIDE, SIDE, 3 * TQ // 2, 2 * HD), bf16),
            pltpu.SemaphoreType.DMA((2, 15)),
            pltpu.SemaphoreType.DMA((2, SIDE)),
            pltpu.SemaphoreType.DMA((2, 6)),
            pltpu.SemaphoreType.DMA((2, 12)),
            pltpu.SemaphoreType.DMA((1 + SIDE,)),
        ],
        cost_estimate=pl.CostEstimate(
            flops=6 * SIDE * rows * width * HD * SIDE, bytes_accessed=8 << 20, transcendentals=0
        ),
        compiler_params=pltpu.CompilerParams(
            collective_id=0, has_side_effects=True, vmem_limit_bytes=32 << 20
        ),
        name="gather_project",
    )(tokens, gain, weights)


def body(
    tokens,
    gain_attn,
    w_qkv,
    w_attn_out,
    kv_cache,
    page_table,
    cached_lengths,
    gain_moe,
    w_router,
    routes,
    w_in,
    w_out,
):
    lanes = lax.axis_size("tensor")
    rows_here = tokens.shape[0]
    out_weights = lax.all_gather(w_attn_out.T, ("batch", "tensor"), axis=0)
    out_weights = out_weights.reshape(-1, lanes * HD, w_attn_out.shape[0])
    blocks = project(tokens, gain_attn.reshape(1, -1), w_qkv.T)
    attended = attention(page_table[0], cached_lengths, blocks, kv_cache)
    shares = lax.all_to_all(attended, "tensor", split_axis=0, concat_axis=0, tiled=True)
    shares = shares.reshape(lanes, TQ // 2, 2, HD).transpose(2, 1, 0, 3).reshape(rows_here, lanes * HD)
    projection = jnp.einsum(
        "tk,bkn->tbn", shares, out_weights, preferred_element_type=jnp.float32
    ).reshape(rows_here, -1)
    state = tokens.astype(jnp.float32) + projection
    normed_moe = rms_norm(state, gain_moe).astype(jnp.bfloat16)
    logits = jnp.dot(normed_moe, w_router, preferred_element_type=jnp.float32)
    experts = w_router.shape[1]
    top_count = routes.shape[1]
    onehot = (routes[:, :, None] == jnp.arange(experts, dtype=jnp.int32)[None, None, :]).astype(
        jnp.int32
    )
    picked = jnp.sum(onehot.astype(jnp.float32) * logits[:, None, :], axis=2)
    squashed = jax.nn.sigmoid(picked)
    gates = squashed / jnp.sum(squashed, axis=1, keepdims=True)
    flat_hits = onehot.reshape(rows_here * top_count, experts)
    before = jnp.cumsum(flat_hits, axis=0) - flat_hits
    slots = jnp.sum(before * flat_hits, axis=1).reshape(rows_here, top_count)
    capacity = max(2, (5 * rows_here * top_count + 4 * experts - 1) // (4 * experts))
    position = routes * capacity + slots
    slot_ids = jnp.arange(experts * capacity, dtype=jnp.int32)
    placing = jnp.any(slot_ids[:, None, None] == position[None, :, :], axis=2).astype(jnp.bfloat16)
    buffer = jnp.dot(placing, normed_moe, preferred_element_type=jnp.float32).astype(jnp.bfloat16)
    buffer = buffer.reshape(lanes, w_in.shape[0], capacity, normed_moe.shape[1])
    width_ff = w_out.shape[1]
    inner = jnp.einsum(
        "sekd,edf->sekf",
        lax.all_to_all(buffer, "tensor", split_axis=0, concat_axis=0, tiled=True),
        w_in,
        preferred_element_type=jnp.float32,
    )
    active = (jax.nn.gelu(inner[..., :width_ff], approximate=True) * inner[..., width_ff:]).astype(
        jnp.bfloat16
    )
    results = jnp.einsum(
        "sekf,efd->sekd", active, w_out, preferred_element_type=jnp.float32
    ).astype(jnp.bfloat16)
    returned = lax.all_to_all(results, "tensor", split_axis=0, concat_axis=0, tiled=True).reshape(
        experts * capacity, normed_moe.shape[1]
    )
    mixed = state
    for rank in range(top_count):
        pick = (position[:, rank : rank + 1] == slot_ids[None, :]).astype(jnp.bfloat16)
        mixed = mixed + gates[:, rank : rank + 1] * jnp.dot(
            pick, returned, preferred_element_type=jnp.float32
        )
    return mixed.astype(jnp.bfloat16)


def solution(mesh):
    in_specs = (
        P(("batch", "tensor"), None),
        P(),
        P("batch", "tensor"),
        P("batch", "tensor"),
        P("batch", None, "tensor"),
        P("batch", None),
        P("batch"),
        P(),
        P(),
        P(("batch", "tensor"), None),
        P("tensor", None, None),
        P("tensor", None, None),
    )
    out_specs = P(("batch", "tensor"), None)
    return jax.shard_map(body, mesh=mesh, in_specs=in_specs, out_specs=out_specs, check_vma=False)
```
